32 devices in a mesh: groups: 2 (over x), seq: 16 (over z, y, core).
Axes of the slice: x: 2, y: 2, z: 4, core: 2. Of those that a mesh axis runs over, the one named last changes fastest.
Arguments:
- features: bfloat16 [16384, 1024], P(('groups', 'seq')), parts along dimension 0, may hold values from -6 to 6
- attention_gain: float32 [1024], replicated, may hold values from 0.1 to 1.9
- qkv_weight: bfloat16 [1024, 3072], replicated, may hold values from -0.1875 to 0.1875
- out_weight: bfloat16 [1024, 1024], replicated, may hold values from -0.1875 to 0.1875
- mlp_gain: float32 [1024], replicated, may hold values from 0.1 to 1.9
- up_weight: bfloat16 [1024, 2048], P(None, 'seq'), may hold values from -0.1875 to 0.1875
- down_weight: bfloat16 [2048, 1024], P('seq'), may hold values from -0.125 to 0.125
- block_columns: int32 [128, 8], P('groups'), parts along dimension 0, may hold values from 0 to 63, as said below
- block_counts: int32 [128], P('groups'), parts along dimension 0, may hold values from 1 to 8, as said below
- global_nodes: int32 [1024], P('groups'), parts along dimension 0, may hold values from 0 to 8191, as said below
Outputs:
- layer_out: bfloat16 [16384, 1024], P(('groups', 'seq')), parts along dimension 0
The draws below stay inside these ranges and needn't reach their ends.
There are 2 independent parts, one for each index of `groups`. The reference program is written for one: setup_inputs(seed, part) draws one part's arguments, and reference() takes and returns one part's arrays. A program takes and returns all parts, laid end to end along the dimension named above; an argument that names none is the same for every part. Nothing has to cross between parts.
Inputs may be any that keep to these rules, and one draw needn't show every extreme that they name: In every row of block_columns the 8 entries are distinct block numbers. `block_counts`: some row block uses all 8 listed column blocks. `global_nodes`: the 512 global nodes are distinct.
All inputs are finite; a program needn't handle non-finite values.
Results may differ from the reference program's by a relative error of at most 0.005.
Values may be sent and summed in bfloat16 or wider, within the bound.
A program may use at most 128 MiB of HBM per device.

```python
import jax
import jax.numpy as jnp
from jax import lax

HEADS = 16
HEAD_DIM = 64
D = 1024
FF = 2048
BLOCK = 128
KMAX = 8
NG = 512
NODES = 8192
NBLK = 64


def draw_block_columns(key, part):
    row_keys = jax.random.split(key, NBLK)
    orders = jax.vmap(lambda row_key: jax.random.permutation(row_key, NBLK))(row_keys)
    offsets = orders[:, :KMAX].astype(jnp.int32)
    rows_ids = jnp.arange(NBLK, dtype=jnp.int32)[:, None]
    return ((rows_ids + offsets) % NBLK).astype(jnp.int32)


def draw_block_counts(key, part):
    counts = jax.random.randint(key, (NBLK,), 1, KMAX + 1, dtype=jnp.int32)
    chosen = jax.random.randint(jax.random.fold_in(key, 7), (), 0, NBLK, dtype=jnp.int32)
    return counts.at[chosen].set(KMAX).astype(jnp.int32)


def draw_global_nodes(key, part):
    return jax.random.permutation(key, NODES)[:NG].astype(jnp.int32)


def level_of(stream_key, shape, cuts, smallest, high):
    loudness, own = 1.0, jax.random.fold_in(stream_key, 6)
    for axis_at, blocks in cuts:
        draws = jnp.exp(jax.random.uniform(jax.random.fold_in(own, axis_at), (blocks,), jnp.float32, smallest / len(cuts), high / len(cuts)))
        loudness = loudness * jnp.repeat(draws, shape[axis_at] // blocks).reshape([-1 if axis == axis_at else 1 for axis in range(len(shape))])
    return loudness


def gaussian(stream_key, extent, width, reach, cuts=(), kind=jnp.bfloat16):
    level = level_of(stream_key, extent, cuts, -0.22, 0.18) if cuts else 1.0
    entries = jax.random.normal(stream_key, extent, jnp.float32) * width * level
    return jnp.minimum(jnp.maximum(entries, -reach), reach).astype(kind)


def setup_inputs(seed: int = 0, part: int = 0) -> dict:
    key_list = jax.random.split(jax.random.key(seed), 11)
    part_splits = jax.random.split(jax.random.fold_in(key_list[10], part), 11)
    features = gaussian(part_splits[0], (NODES, D), 1.0, 6.0, ((0, 16),))
    attention_gain = jnp.clip(1.0 + 0.18 * jax.random.normal(key_list[1], (D,), jnp.float32), 0.1, 1.9)
    qkv_weight = gaussian(key_list[2], (D, 3 * D), D ** -0.5, 0.1875)
    out_weight = gaussian(key_list[3], (D, D), D ** -0.5, 0.1875)
    mlp_gain = jnp.clip(1.0 + 0.18 * jax.random.normal(key_list[4], (D,), jnp.float32), 0.1, 1.9)
    up_weight = gaussian(key_list[5], (D, FF), D ** -0.5, 0.1875, ((1, 16),))
    down_weight = gaussian(key_list[6], (FF, D), FF ** -0.5, 0.125, ((0, 16),))
    block_columns = draw_block_columns(jax.random.fold_in(jax.random.fold_in(key_list[10], part), 71), part)
    block_counts = draw_block_counts(jax.random.fold_in(jax.random.fold_in(key_list[10], part), 71), part)
    global_nodes = draw_global_nodes(jax.random.fold_in(jax.random.fold_in(key_list[10], part), 71), part)
    return {"features": features, "attention_gain": attention_gain, "qkv_weight": qkv_weight, "out_weight": out_weight, "mlp_gain": mlp_gain, "up_weight": up_weight, "down_weight": down_weight, "block_columns": block_columns, "block_counts": block_counts, "global_nodes": global_nodes}


EPS = 1e-05

def layer_norm(values, gain):
    values = values.astype(jnp.float32)
    average = lax.optimization_barrier(jnp.mean(values, axis=-1, keepdims=True))
    centered = values - average
    variance = lax.optimization_barrier(jnp.mean(centered * centered, axis=-1, keepdims=True))
    return centered * lax.rsqrt(variance + EPS) * gain.astype(jnp.float32)

def attend_group(queries, memory_blocks, memory_global, global_block, columns, counts):
    groups, block_rows, head_dim = queries.shape
    slot_count = columns.shape[1]
    in_list = jnp.arange(slot_count, dtype=jnp.int32)[None, :] < counts[:, None]
    picked = memory_blocks[columns].reshape(groups, slot_count * block_rows, 2 * head_dim)
    key_local = picked[:, :, :head_dim].astype(jnp.float32)
    value_local = picked[:, :, head_dim:].astype(jnp.float32)
    query_float = queries.astype(jnp.float32)
    score_scale = head_dim ** (-0.5)
    local_scores = jnp.einsum('gqd,gkd->gqk', query_float, key_local) * score_scale
    key_mask = jnp.repeat(in_list, block_rows, axis=1)[:, None, :]
    local_weights = jnp.where(key_mask, jnp.exp(local_scores), 0.0)
    duplicate = jnp.any(in_list[:, :, None] & (columns[:, :, None] == global_block[None, None, :]), axis=1)
    global_scores = jnp.einsum('gqd,nd->gqn', query_float, memory_global[:, :head_dim].astype(jnp.float32)) * score_scale
    global_weights = jnp.where(duplicate[:, None, :], 0.0, jnp.exp(global_scores))
    totals = lax.optimization_barrier(jnp.sum(local_weights, axis=-1, keepdims=True)) + lax.optimization_barrier(jnp.sum(global_weights, axis=-1, keepdims=True))
    local_probs = (local_weights / totals).astype(jnp.bfloat16)
    global_probs = (global_weights / totals).astype(jnp.bfloat16)
    result = jnp.einsum('gqk,gkd->gqd', local_probs.astype(jnp.float32), value_local)
    result = result + jnp.einsum('gqn,nd->gqd', global_probs.astype(jnp.float32), memory_global[:, head_dim:].astype(jnp.float32))
    return result.astype(jnp.bfloat16)

def reference(features, attention_gain, qkv_weight, out_weight, mlp_gain, up_weight, down_weight, block_columns, block_counts, global_nodes):
    normed = layer_norm(features, attention_gain).astype(jnp.bfloat16)
    packed = jnp.dot(normed, qkv_weight, preferred_element_type=jnp.float32).astype(jnp.bfloat16)
    queries = packed[:, :D].reshape(NODES, HEADS, HEAD_DIM).transpose(1, 0, 2)
    keys_all = packed[:, D:2 * D].reshape(NODES, HEADS, HEAD_DIM)
    values_all = packed[:, 2 * D:].reshape(NODES, HEADS, HEAD_DIM)
    memory_heads = jnp.concatenate((keys_all, values_all), axis=2).transpose(1, 0, 2)
    global_block = (global_nodes // BLOCK).astype(jnp.int32)
    turns = NBLK // 4
    column_groups = block_columns.reshape(turns, 4, KMAX)
    count_groups = block_counts.reshape(turns, 4)

    def one_head(head_pair):
        query_head, memory_head = head_pair
        memory_blocks = memory_head.reshape(NBLK, BLOCK, 2 * HEAD_DIM)
        memory_global = memory_head[global_nodes]
        query_groups = query_head.reshape(turns, 4, BLOCK, HEAD_DIM)

        def one_group(group_item):
            return attend_group(group_item[0], memory_blocks, memory_global, global_block, group_item[1], group_item[2])
        return lax.map(one_group, (query_groups, column_groups, count_groups)).reshape(NODES, HEAD_DIM)
    attended = lax.map(one_head, (queries, memory_heads))
    attended = attended.transpose(1, 0, 2).reshape(NODES, D)
    mixed_rows = features.astype(jnp.float32) + jnp.dot(attended, out_weight, preferred_element_type=jnp.float32)
    normed_mlp = layer_norm(mixed_rows, mlp_gain).astype(jnp.bfloat16)
    hidden = jax.nn.gelu(jnp.dot(normed_mlp, up_weight, preferred_element_type=jnp.float32), approximate=True).astype(jnp.bfloat16)
    return (mixed_rows + jnp.dot(hidden, down_weight, preferred_element_type=jnp.float32)).astype(jnp.bfloat16)
```

```python
import functools

import jax
import jax.numpy as jnp
from jax import lax
from jax.experimental import pallas as pl
from jax.experimental.pallas import tpu as pltpu
from jax.sharding import PartitionSpec as P

HEADS = 16
BLOCK = 128
EPS = 1e-05
MASKED = -1e30


def layer_norm(values, gain):
    values = values.astype(jnp.float32)
    average = jnp.mean(values, axis=-1, keepdims=True)
    centered = values - average
    variance = jnp.mean(centered * centered, axis=-1, keepdims=True)
    return centered * lax.rsqrt(variance + EPS) * gain


def swap_halves(left, right):
    low = lax.broadcasted_iota(jnp.int32, left.shape, 1) < 64
    return (
        jnp.where(low, left, pltpu.roll(right, 64, 1)),
        jnp.where(low, pltpu.roll(left, 64, 1), right),
    )


def attention_kernel(
    n,
    repeat,
    x_ref,
    gain_ref,
    w_ref,
    bias_ref,
    gidx_ref,
    cols_ref,
    out_ref,
    normed,
    kv_out,
    memory,
    q_out,
    q_in,
    o_out,
    o_in,
    global_sum,
    global_kv,
    kv_send,
    kv_recv,
    q_send,
    q_recv,
    o_send,
    o_recv,
):
    rows, width = x_ref.shape
    sub_rows = rows // repeat
    half = sub_rows // 2
    blocks = rows // BLOCK
    slots = cols_ref.shape[1]
    me = lax.axis_index("seq")
    my_head, my_sub = me // repeat, me % repeat
    f32, bf16 = jnp.float32, jnp.bfloat16

    barrier = pltpu.get_barrier_semaphore()

    def greet(step, carry):
        peer = (me + step) % n
        pl.semaphore_signal(
            barrier, inc=1, device_id={"seq": peer}, device_id_type=pl.DeviceIdType.MESH
        )
        return carry

    lax.fori_loop(1, n, greet, 0)

    def kv_copy(head, owner, source):
        return pltpu.make_async_remote_copy(
            src_ref=kv_out.at[head],
            dst_ref=memory.at[pl.ds(source * blocks, blocks)],
            send_sem=kv_send.at[owner],
            recv_sem=kv_recv.at[source],
            device_id={"seq": owner},
            device_id_type=pl.DeviceIdType.MESH,
        )

    def q_copy(owner, source):
        return pltpu.make_async_remote_copy(
            src_ref=q_out.at[owner],
            dst_ref=q_in.at[source],
            send_sem=q_send.at[owner],
            recv_sem=q_recv.at[source],
            device_id={"seq": owner},
            device_id_type=pl.DeviceIdType.MESH,
        )

    def o_copy(home, worker):
        return pltpu.make_async_remote_copy(
            src_ref=o_out.at[home],
            dst_ref=o_in.at[worker],
            send_sem=o_send.at[home],
            recv_sem=o_recv.at[worker],
            device_id={"seq": home},
            device_id_type=pl.DeviceIdType.MESH,
        )

    def norm_rows(i, carry):
        at = pl.ds(pl.multiple_of(i * BLOCK, BLOCK), BLOCK)
        normed[at, :] = layer_norm(x_ref[at, :], gain_ref[...]).astype(bf16)
        return carry

    lax.fori_loop(0, rows // BLOCK, norm_rows, 0)
    pl.semaphore_wait(barrier, n - 1)

    def quad_of(i):
        return (me // (4 * repeat) + 1 + i) % (HEADS // 4)

    def project(first, quad):
        columns = pl.ds(pl.multiple_of(first * width + quad * 256, 256), 256)
        return jnp.dot(normed[...], w_ref[:, columns], preferred_element_type=f32)

    def kv_quad(i, carry):
        quad = quad_of(i)
        keys = project(1, quad)
        values = project(2, quad)
        for pair in range(2):
            at = slice(pair * 128, pair * 128 + 128)
            first, second = swap_halves(keys[:, at], values[:, at])
            kv_out[quad * 4 + 2 * pair] = first.astype(bf16).reshape(blocks, BLOCK, 128)
            kv_out[quad * 4 + 2 * pair + 1] = second.astype(bf16).reshape(blocks, BLOCK, 128)
        for inner in range(4):
            head = quad * 4 + inner
            for sub in range(repeat):
                owner = head * repeat + sub

                @pl.when(owner != me)
                def _():
                    kv_copy(head, owner, me).start()

        return carry

    lax.fori_loop(0, HEADS // 4, kv_quad, 0)

    def q_quad(i, carry):
        quad = quad_of(i)
        queries = project(0, quad) * 0.125
        for pair in range(2):
            both = queries[:, pair * 128 : pair * 128 + 128]
            for sub in range(repeat):
                top = both[sub * sub_rows : sub * sub_rows + half]
                bottom = both[sub * sub_rows + half : (sub + 1) * sub_rows]
                first, second = swap_halves(top, bottom)
                head = quad * 4 + 2 * pair
                q_out[head * repeat + sub] = first.astype(bf16)
                q_out[(head + 1) * repeat + sub] = second.astype(bf16)
        for inner in range(4):
            for sub in range(repeat):
                owner = (quad * 4 + inner) * repeat + sub

                @pl.when(owner != me)
                def _():
                    q_copy(owner, me).start()

        return carry

    lax.fori_loop(0, HEADS // 4, q_quad, 0)

    memory[pl.ds(me * blocks, blocks)] = kv_out[my_head]
    q_in[me] = q_out[me]

    global_sum[...] = jnp.zeros_like(global_sum)

    def arrive(step, carry):
        source = (me + n - step) % n

        @pl.when(source != me)
        def _():
            kv_copy(my_head, me, source).wait_recv()

        offset = gidx_ref[...] - source * rows
        spot = lax.broadcasted_iota(jnp.int32, (offset.shape[0], rows), 1)
        chosen = jnp.where(spot == offset, 1.0, 0.0).astype(bf16)
        chunk = memory[pl.ds(source * blocks, blocks)].reshape(rows, 128)
        global_sum[...] += jnp.dot(chosen, chunk, preferred_element_type=f32)
        return carry

    lax.fori_loop(0, n, arrive, 0)
    global_kv[...] = global_sum[...].astype(bf16)

    def serve(step, carry):
        source = (me + n - step) % n

        @pl.when(source != me)
        def _():
            q_copy(me, source).wait_recv()

        packed = q_in[source].astype(f32)
        low = lax.broadcasted_iota(jnp.int32, packed.shape, 1) < 64
        top = jnp.where(low, packed, 0.0).astype(bf16)
        bottom = jnp.where(low, pltpu.roll(packed, 64, 1), 0.0).astype(bf16)
        queries = jnp.concatenate((top, bottom), axis=0)
        results = []
        for r in range(sub_rows // BLOCK):
            block = source * (rows // BLOCK) + my_sub * (sub_rows // BLOCK) + r
            picked = [memory[cols_ref[block, j]] for j in range(slots)]
            kv = jnp.concatenate(picked + [global_kv[...]], axis=0)
            scores = lax.dot_general(
                queries[r * BLOCK : (r + 1) * BLOCK],
                kv,
                (((1,), (1,)), ((), ())),
                preferred_element_type=f32,
            )
            weights = jnp.exp(scores + bias_ref[pl.ds(block, 1), :])
            totals = jnp.sum(weights, axis=1, keepdims=True)
            scale = jnp.where(totals > 1.0, 2.0**-10, 1.0)
            probs = (weights * (1.0 / (totals * scale))).astype(bf16)
            results.append(jnp.dot(probs, kv, preferred_element_type=f32) * scale)
        result = jnp.concatenate(results, axis=0)
        top, bottom = result[:half], result[half:]
        o_out[source] = jnp.where(low, pltpu.roll(top, 64, 1), bottom).astype(bf16)

        @pl.when(source != me)
        def _():
            o_copy(source, me).start()

        return carry

    lax.fori_loop(0, n, serve, 0)
    o_in[me] = o_out[me]

    def settle(step, carry):
        peer = (me + step) % n
        o_copy(me, peer).wait_recv()
        kv_copy(peer // repeat, peer, me).wait_send()
        q_copy(peer, me).wait_send()
        o_copy(peer, me).wait_send()
        return carry

    lax.fori_loop(1, n, settle, 0)

    for pair in range(HEADS // 2):
        for sub in range(repeat):
            first = o_in[2 * pair * repeat + sub].astype(f32)
            second = o_in[(2 * pair + 1) * repeat + sub].astype(f32)
            top, bottom = swap_halves(first, second)
            at = slice(pair * 128, pair * 128 + 128)
            out_ref[sub * sub_rows : sub * sub_rows + half, at] = top.astype(bf16)
            out_ref[sub * sub_rows + half : (sub + 1) * sub_rows, at] = bottom.astype(bf16)


def attend(features, gain, weight, bias, global_nodes, columns):
    n = lax.axis_size("seq")
    repeat = n // HEADS
    rows, width = features.shape
    half = rows // repeat // 2
    globals_count = global_nodes.shape[0]
    bf16 = jnp.bfloat16
    vmem = pl.BlockSpec(memory_space=pltpu.VMEM)
    flops = 2 * rows * width * 3 * width + 4 * rows * HEADS * 64 * bias.shape[1]
    return pl.pallas_call(
        functools.partial(attention_kernel, n, repeat),
        out_shape=jax.ShapeDtypeStruct((rows, width), bf16),
        in_specs=[vmem] * 5 + [pl.BlockSpec(memory_space=pltpu.SMEM)],
        out_specs=vmem,
        scratch_shapes=[
            pltpu.VMEM((rows, width), bf16),
            pltpu.VMEM((HEADS, rows // BLOCK, BLOCK, 128), bf16),
            pltpu.VMEM((n * rows // BLOCK, BLOCK, 128), bf16),
            pltpu.VMEM((n, half, 128), bf16),
            pltpu.VMEM((n, half, 128), bf16),
            pltpu.VMEM((n, half, 128), bf16),
            pltpu.VMEM((n, half, 128), bf16),
            pltpu.VMEM((globals_count, 128), jnp.float32),
            pltpu.VMEM((globals_count, 128), bf16),
        ]
        + [pltpu.SemaphoreType.DMA((n,))] * 6,
        compiler_params=pltpu.CompilerParams(
            collective_id=0, has_side_effects=True, vmem_limit_bytes=48 * 2**20
        ),
        cost_estimate=pl.CostEstimate(
            flops=flops * 16, bytes_accessed=2**24, transcendentals=rows * HEADS * bias.shape[1]
        ),
        name="attend",
    )(features, gain[None, :], weight, bias, global_nodes[:, None], columns)


def on_device(
    features,
    attention_gain,
    qkv_weight,
    out_weight,
    mlp_gain,
    up_weight,
    down_weight,
    block_columns,
    block_counts,
    global_nodes,
):
    slots = block_columns.shape[1]
    in_list = jnp.arange(slots, dtype=jnp.int32)[None, :] < block_counts[:, None]
    global_block = global_nodes // BLOCK
    duplicate = jnp.any(
        in_list[:, :, None] & (block_columns[:, :, None] == global_block[None, None, :]), axis=1
    )
    bias = jnp.concatenate(
        (
            jnp.repeat(jnp.where(in_list, 0.0, MASKED), BLOCK, axis=1),
            jnp.where(duplicate, MASKED, 0.0),
        ),
        axis=1,
    ).astype(jnp.float32)
    attended_rows = attend(
        features, attention_gain, qkv_weight, bias, global_nodes, block_columns
    )
    mixed_rows = features.astype(jnp.float32) + jnp.dot(
        attended_rows, out_weight, preferred_element_type=jnp.float32
    )
    normed_mlp = layer_norm(mixed_rows, mlp_gain).astype(jnp.bfloat16)
    hidden = jax.nn.gelu(
        jnp.dot(
            normed_mlp,
            lax.all_gather(up_weight, "seq", axis=1, tiled=True),
            preferred_element_type=jnp.float32,
        ),
        approximate=True,
    ).astype(jnp.bfloat16)
    reduced = jnp.dot(
        hidden,
        lax.all_gather(down_weight, "seq", axis=0, tiled=True),
        preferred_element_type=jnp.float32,
    )
    return (mixed_rows + reduced).astype(jnp.bfloat16)


def solution(mesh):
    in_specs = (
        P(("groups", "seq"), None),
        P(),
        P(),
        P(),
        P(),
        P(None, "seq"),
        P("seq", None),
        P("groups", None),
        P("groups"),
        P("groups"),
    )
    out_specs = P(("groups", "seq"), None)
    return jax.shard_map(
        on_device, mesh=mesh, in_specs=in_specs, out_specs=out_specs, check_vma=False
    )
```

```python
import functools

import jax
import jax.numpy as jnp
from jax import lax
from jax.experimental import pallas as pl
from jax.experimental.pallas import tpu as pltpu
from jax.sharding import PartitionSpec as P

HEADS = 16
BLOCK = 128
EPS = 1e-05
MASKED = -1e30


def layer_norm(values, gain):
    values = values.astype(jnp.float32)
    average = jnp.mean(values, axis=-1, keepdims=True)
    centered = values - average
    variance = jnp.mean(centered * centered, axis=-1, keepdims=True)
    return centered * lax.rsqrt(variance + EPS) * gain


def swap_halves(left, right):
    low = lax.broadcasted_iota(jnp.int32, left.shape, 1) < 64
    return (
        jnp.where(low, left, pltpu.roll(right, 64, 1)),
        jnp.where(low, pltpu.roll(left, 64, 1), right),
    )


def attention_kernel(
    n,
    repeat,
    x_ref,
    gain_ref,
    w_ref,
    bias_ref,
    gidx_ref,
    cols_ref,
    out_ref,
    normed,
    kv_out,
    memory,
    q_out,
    q_in,
    o_out,
    o_in,
    global_sum,
    global_kv,
    kv_send,
    kv_recv,
    q_send,
    q_recv,
    o_send,
    o_recv,
):
    rows, width = x_ref.shape
    sub_rows = rows // repeat
    half = sub_rows // 2
    blocks = rows // BLOCK
    slots = cols_ref.shape[1]
    me = lax.axis_index("seq")
    my_head, my_sub = me // repeat, me % repeat
    f32, bf16 = jnp.float32, jnp.bfloat16

    barrier = pltpu.get_barrier_semaphore()

    def greet(step, carry):
        peer = (me + step) % n
        pl.semaphore_signal(
            barrier, inc=1, device_id={"seq": peer}, device_id_type=pl.DeviceIdType.MESH
        )
        return carry

    lax.fori_loop(1, n, greet, 0)

    def kv_copy(head, owner, source):
        return pltpu.make_async_remote_copy(
            src_ref=kv_out.at[head],
            dst_ref=memory.at[pl.ds(source * blocks, blocks)],
            send_sem=kv_send.at[owner],
            recv_sem=kv_recv.at[source],
            device_id={"seq": owner},
            device_id_type=pl.DeviceIdType.MESH,
        )

    def q_copy(owner, source):
        return pltpu.make_async_remote_copy(
            src_ref=q_out.at[owner],
            dst_ref=q_in.at[source],
            send_sem=q_send.at[owner],
            recv_sem=q_recv.at[source],
            device_id={"seq": owner},
            device_id_type=pl.DeviceIdType.MESH,
        )

    def o_copy(home, worker):
        return pltpu.make_async_remote_copy(
            src_ref=o_out.at[home],
            dst_ref=o_in.at[worker],
            send_sem=o_send.at[home],
            recv_sem=o_recv.at[worker],
            device_id={"seq": home},
            device_id_type=pl.DeviceIdType.MESH,
        )

    def norm_rows(i, carry):
        at = pl.ds(pl.multiple_of(i * BLOCK, BLOCK), BLOCK)
        normed[at, :] = layer_norm(x_ref[at, :], gain_ref[...]).astype(bf16)
        return carry

    lax.fori_loop(0, rows // BLOCK, norm_rows, 0)
    pl.semaphore_wait(barrier, n - 1)

    def quad_of(i):
        return (me // (4 * repeat) + 1 + i) % (HEADS // 4)

    def project(first, quad):
        columns = pl.ds(pl.multiple_of(first * width + quad * 256, 256), 256)
        return jnp.dot(normed[...], w_ref[:, columns], preferred_element_type=f32)

    def kv_quad(i, carry):
        quad = quad_of(i)
        keys = project(1, quad)
        values = project(2, quad)
        for pair in range(2):
            at = slice(pair * 128, pair * 128 + 128)
            first, second = swap_halves(keys[:, at], values[:, at])
            kv_out[quad * 4 + 2 * pair] = first.astype(bf16).reshape(blocks, BLOCK, 128)
            kv_out[quad * 4 + 2 * pair + 1] = second.astype(bf16).reshape(blocks, BLOCK, 128)
        for inner in range(4):
            head = quad * 4 + inner
            for sub in range(repeat):
                owner = head * repeat + sub

                @pl.when(owner != me)
                def _():
                    kv_copy(head, owner, me).start()

        return carry

    lax.fori_loop(0, HEADS // 4, kv_quad, 0)

    def q_quad(i, carry):
        quad = quad_of(i)
        queries = project(0, quad) * 0.125
        for pair in range(2):
            both = queries[:, pair * 128 : pair * 128 + 128]
            for sub in range(repeat):
                top = both[sub * sub_rows : sub * sub_rows + half]
                bottom = both[sub * sub_rows + half : (sub + 1) * sub_rows]
                first, second = swap_halves(top, bottom)
                head = quad * 4 + 2 * pair
                q_out[head * repeat + sub] = first.astype(bf16)
                q_out[(head + 1) * repeat + sub] = second.astype(bf16)
        for inner in range(4):
            for sub in range(repeat):
                owner = (quad * 4 + inner) * repeat + sub

                @pl.when(owner != me)
                def _():
                    q_copy(owner, me).start()

        return carry

    lax.fori_loop(0, HEADS // 4, q_quad, 0)

    memory[pl.ds(me * blocks, blocks)] = kv_out[my_head]
    q_in[me] = q_out[me]

    global_sum[...] = jnp.zeros_like(global_sum)

    def arrive(step, carry):
        source = (me + n - step) % n

        @pl.when(source != me)
        def _():
            kv_copy(my_head, me, source).wait_recv()

        offset = gidx_ref[...] - source * rows
        spot = lax.broadcasted_iota(jnp.int32, (offset.shape[0], rows), 1)
        chosen = jnp.where(spot == offset, 1.0, 0.0).astype(bf16)
        chunk = memory[pl.ds(source * blocks, blocks)].reshape(rows, 128)
        global_sum[...] += jnp.dot(chosen, chunk, preferred_element_type=f32)
        return carry

    lax.fori_loop(0, n, arrive, 0)
    global_kv[...] = global_sum[...].astype(bf16)

    def serve(step, carry):
        source = (me + n - step) % n

        @pl.when(source != me)
        def _():
            q_copy(me, source).wait_recv()

        packed = q_in[source].astype(f32)
        low = lax.broadcasted_iota(jnp.int32, packed.shape, 1) < 64
        top = jnp.where(low, packed, 0.0).astype(bf16)
        bottom = jnp.where(low, pltpu.roll(packed, 64, 1), 0.0).astype(bf16)
        queries = jnp.concatenate((top, bottom), axis=0)
        results = []
        for r in range(sub_rows // BLOCK):
            block = source * (rows // BLOCK) + my_sub * (sub_rows // BLOCK) + r
            picked = [memory[cols_ref[block, j]] for j in range(slots)]
            kv = jnp.concatenate(picked + [global_kv[...]], axis=0)
            scores = lax.dot_general(
                queries[r * BLOCK : (r + 1) * BLOCK],
                kv,
                (((1,), (1,)), ((), ())),
                preferred_element_type=f32,
            )
            weights = jnp.exp(scores + bias_ref[pl.ds(block, 1), :])
            totals = jnp.sum(weights, axis=1, keepdims=True)
            scale = jnp.where(totals > 1.0, 2.0**-10, 1.0)
            probs = (weights * (1.0 / (totals * scale))).astype(bf16)
            results.append(jnp.dot(probs, kv, preferred_element_type=f32) * scale)
        result = jnp.concatenate(results, axis=0)
        top, bottom = result[:half], result[half:]
        o_out[source] = jnp.where(low, pltpu.roll(top, 64, 1), bottom).astype(bf16)

        @pl.when(source != me)
        def _():
            o_copy(source, me).start()

        return carry

    lax.fori_loop(0, n, serve, 0)
    o_in[me] = o_out[me]

    def settle(step, carry):
        peer = (me + step) % n
        o_copy(me, peer).wait_recv()
        kv_copy(peer // repeat, peer, me).wait_send()
        q_copy(peer, me).wait_send()
        o_copy(peer, me).wait_send()
        return carry

    lax.fori_loop(1, n, settle, 0)

    for pair in range(HEADS // 2):
        for sub in range(repeat):
            first = o_in[2 * pair * repeat + sub].astype(f32)
            second = o_in[(2 * pair + 1) * repeat + sub].astype(f32)
            top, bottom = swap_halves(first, second)
            at = slice(pair * 128, pair * 128 + 128)
            out_ref[sub * sub_rows : sub * sub_rows + half, at] = top.astype(bf16)
            out_ref[sub * sub_rows + half : (sub + 1) * sub_rows, at] = bottom.astype(bf16)


def attend(features, gain, weight, bias, global_nodes, columns):
    n = lax.axis_size("seq")
    repeat = n // HEADS
    rows, width = features.shape
    half = rows // repeat // 2
    globals_count = global_nodes.shape[0]
    bf16 = jnp.bfloat16
    vmem = pl.BlockSpec(memory_space=pltpu.VMEM)
    flops = 2 * rows * width * 3 * width + 4 * rows * HEADS * 64 * bias.shape[1]
    return pl.pallas_call(
        functools.partial(attention_kernel, n, repeat),
        out_shape=jax.ShapeDtypeStruct((rows, width), bf16),
        in_specs=[vmem] * 5 + [pl.BlockSpec(memory_space=pltpu.SMEM)],
        out_specs=vmem,
        scratch_shapes=[
            pltpu.VMEM((rows, width), bf16),
            pltpu.VMEM((HEADS, rows // BLOCK, BLOCK, 128), bf16),
            pltpu.VMEM((n * rows // BLOCK, BLOCK, 128), bf16),
            pltpu.VMEM((n, half, 128), bf16),
            pltpu.VMEM((n, half, 128), bf16),
            pltpu.VMEM((n, half, 128), bf16),
            pltpu.VMEM((n, half, 128), bf16),
            pltpu.VMEM((globals_count, 128), jnp.float32),
            pltpu.VMEM((globals_count, 128), bf16),
        ]
        + [pltpu.SemaphoreType.DMA((n,))] * 6,
        compiler_params=pltpu.CompilerParams(
            collective_id=0, has_side_effects=True, vmem_limit_bytes=48 * 2**20
        ),
        cost_estimate=pl.CostEstimate(
            flops=flops * 16, bytes_accessed=2**24, transcendentals=rows * HEADS * bias.shape[1]
        ),
        name="attend",
    )(features, gain[None, :], weight, bias, global_nodes[:, None], columns)


def on_device(
    features,
    attention_gain,
    qkv_weight,
    out_weight,
    mlp_gain,
    up_weight,
    down_weight,
    block_columns,
    block_counts,
    global_nodes,
):
    slots = block_columns.shape[1]
    in_list = jnp.arange(slots, dtype=jnp.int32)[None, :] < block_counts[:, None]
    global_block = global_nodes // BLOCK
    duplicate = jnp.any(
        in_list[:, :, None] & (block_columns[:, :, None] == global_block[None, None, :]), axis=1
    )
    bias = jnp.concatenate(
        (
            jnp.repeat(jnp.where(in_list, 0.0, MASKED), BLOCK, axis=1),
            jnp.where(duplicate, MASKED, 0.0),
        ),
        axis=1,
    ).astype(jnp.float32)
    groups = lax.axis_size("groups")
    part = up_weight.shape[1] // groups
    first = lax.axis_index("groups") * part
    shard = jnp.concatenate(
        (
            lax.dynamic_slice_in_dim(up_weight.T, first, part, 0)[None],
            lax.dynamic_slice_in_dim(down_weight, first, part, 0)[None],
        ),
        axis=0,
    )
    gathered = lax.all_gather(shard, ("seq", "groups"), axis=1, tiled=True)
    up_rows, down_rows = gathered[0], gathered[1]
    attended_rows = attend(
        features, attention_gain, qkv_weight, bias, global_nodes, block_columns
    )
    mixed_rows = features.astype(jnp.float32) + jnp.dot(
        attended_rows, out_weight, preferred_element_type=jnp.float32
    )
    normed_mlp = layer_norm(mixed_rows, mlp_gain).astype(jnp.bfloat16)
    hidden = jax.nn.gelu(
        lax.dot_general(
            normed_mlp,
            up_rows,
            (((1,), (1,)), ((), ())),
            preferred_element_type=jnp.float32,
        ),
        approximate=True,
    ).astype(jnp.bfloat16)
    reduced = jnp.dot(
        hidden,
        down_rows,
        preferred_element_type=jnp.float32,
    )
    return (mixed_rows + reduced).astype(jnp.bfloat16)


def solution(mesh):
    in_specs = (
        P(("groups", "seq"), None),
        P(),
        P(),
        P(),
        P(),
        P(None, "seq"),
        P("seq", None),
        P("groups", None),
        P("groups"),
        P("groups"),
    )
    out_specs = P(("groups", "seq"), None)
    return jax.shard_map(
        on_device, mesh=mesh, in_specs=in_specs, out_specs=out_specs, check_vma=False
    )
```

```python
import functools

import jax
import jax.numpy as jnp
from jax import lax
from jax.experimental import pallas as pl
from jax.experimental.pallas import tpu as pltpu
from jax.sharding import PartitionSpec as P

HEADS = 16
BLOCK = 128
EPS = 1e-05
MASKED = -1e30


def layer_norm(values, gain):
    values = values.astype(jnp.float32)
    average = jnp.mean(values, axis=-1, keepdims=True)
    centered = values - average
    variance = jnp.mean(centered * centered, axis=-1, keepdims=True)
    return centered * lax.rsqrt(variance + EPS) * gain


def swap_halves(left, right):
    low = lax.broadcasted_iota(jnp.int32, left.shape, 1) < 64
    return (
        jnp.where(low, left, pltpu.roll(right, 64, 1)),
        jnp.where(low, pltpu.roll(left, 64, 1), right),
    )


def attention_kernel(
    n,
    repeat,
    x_ref,
    gain_ref,
    w_ref,
    used_ref,
    spots_ref,
    gidx_ref,
    cols_ref,
    out_ref,
    normed,
    kv_out,
    memory,
    q_out,
    q_in,
    o_out,
    o_in,
    global_sum,
    global_kv,
    bias,
    kv_send,
    kv_recv,
    q_send,
    q_recv,
    o_send,
    o_recv,
):
    rows, width = x_ref.shape
    sub_rows = rows // repeat
    half = sub_rows // 2
    blocks = rows // BLOCK
    slots = cols_ref.shape[1]
    me = lax.axis_index("seq")
    my_head, my_sub = me // repeat, me % repeat
    f32, bf16 = jnp.float32, jnp.bfloat16

    barrier = pltpu.get_barrier_semaphore()

    def greet(step, carry):
        peer = (me + step) % n
        pl.semaphore_signal(
            barrier, inc=1, device_id={"seq": peer}, device_id_type=pl.DeviceIdType.MESH
        )
        return carry

    lax.fori_loop(1, n, greet, 0)

    def kv_copy(head, owner, source):
        return pltpu.make_async_remote_copy(
            src_ref=kv_out.at[head],
            dst_ref=memory.at[pl.ds(source * blocks, blocks)],
            send_sem=kv_send.at[owner],
            recv_sem=kv_recv.at[source],
            device_id={"seq": owner},
            device_id_type=pl.DeviceIdType.MESH,
        )

    def q_copy(owner, source):
        return pltpu.make_async_remote_copy(
            src_ref=q_out.at[owner],
            dst_ref=q_in.at[source],
            send_sem=q_send.at[owner],
            recv_sem=q_recv.at[source],
            device_id={"seq": owner},
            device_id_type=pl.DeviceIdType.MESH,
        )

    def o_copy(home, worker):
        return pltpu.make_async_remote_copy(
            src_ref=o_out.at[home],
            dst_ref=o_in.at[worker],
            send_sem=o_send.at[home],
            recv_sem=o_recv.at[worker],
            device_id={"seq": home},
            device_id_type=pl.DeviceIdType.MESH,
        )

    def norm_rows(i, carry):
        at = pl.ds(pl.multiple_of(i * BLOCK, BLOCK), BLOCK)
        normed[at, :] = layer_norm(x_ref[at, :], gain_ref[...]).astype(bf16)
        return carry

    lax.fori_loop(0, rows // BLOCK, norm_rows, 0)
    pl.semaphore_wait(barrier, n - 1)

    def quad_of(i):
        return (me // (4 * repeat) + 1 + i) % (HEADS // 4)

    def project(first, quad):
        columns = pl.ds(pl.multiple_of(first * width + quad * 256, 256), 256)
        return jnp.dot(normed[...], w_ref[:, columns], preferred_element_type=f32)

    def kv_quad(i, carry):
        quad = quad_of(i)
        keys = project(1, quad)
        values = project(2, quad)
        for pair in range(2):
            at = slice(pair * 128, pair * 128 + 128)
            first, second = swap_halves(keys[:, at], values[:, at])
            kv_out[quad * 4 + 2 * pair] = first.astype(bf16).reshape(blocks, BLOCK, 128)
            kv_out[quad * 4 + 2 * pair + 1] = second.astype(bf16).reshape(blocks, BLOCK, 128)
        for inner in range(4):
            head = quad * 4 + inner
            for sub in range(repeat):
                owner = head * repeat + sub

                @pl.when(owner != me)
                def _():
                    kv_copy(head, owner, me).start()

        return carry

    lax.fori_loop(0, HEADS // 4, kv_quad, 0)

    def q_quad(i, carry):
        quad = quad_of(i)
        queries = project(0, quad) * 0.125
        for pair in range(2):
            both = queries[:, pair * 128 : pair * 128 + 128]
            for sub in range(repeat):
                top = both[sub * sub_rows : sub * sub_rows + half]
                bottom = both[sub * sub_rows + half : (sub + 1) * sub_rows]
                first, second = swap_halves(top, bottom)
                head = quad * 4 + 2 * pair
                q_out[head * repeat + sub] = first.astype(bf16)
                q_out[(head + 1) * repeat + sub] = second.astype(bf16)
        for inner in range(4):
            for sub in range(repeat):
                owner = (quad * 4 + inner) * repeat + sub

                @pl.when(owner != me)
                def _():
                    q_copy(owner, me).start()

        return carry

    lax.fori_loop(0, HEADS // 4, q_quad, 0)

    memory[pl.ds(me * blocks, blocks)] = kv_out[my_head]
    q_in[me] = q_out[me]

    used = used_ref[...]
    global_block = lax.shift_right_logical(spots_ref[...], BLOCK.bit_length() - 1)
    excluded = jnp.zeros((used.shape[0], global_block.shape[1]), f32)
    for j in range(slots):
        listed = used[:, j : j + 1]
        excluded = jnp.where(listed == global_block, MASKED, excluded)
        bias[:, j * BLOCK : (j + 1) * BLOCK] = jnp.broadcast_to(
            jnp.where(listed >= 0, 0.0, MASKED), (used.shape[0], BLOCK)
        )
    bias[:, slots * BLOCK :] = excluded

    global_sum[...] = jnp.zeros_like(global_sum)

    def arrive(step, carry):
        source = (me + n - step) % n

        @pl.when(source != me)
        def _():
            kv_copy(my_head, me, source).wait_recv()

        offset = gidx_ref[...] - source * rows
        spot = lax.broadcasted_iota(jnp.int32, (offset.shape[0], rows), 1)
        chosen = jnp.where(spot == offset, 1.0, 0.0).astype(bf16)
        chunk = memory[pl.ds(source * blocks, blocks)].reshape(rows, 128)
        global_sum[...] += jnp.dot(chosen, chunk, preferred_element_type=f32)
        return carry

    lax.fori_loop(0, n, arrive, 0)
    global_kv[...] = global_sum[...].astype(bf16)

    def serve(step, carry):
        source = (me + n - step) % n

        @pl.when(source != me)
        def _():
            q_copy(me, source).wait_recv()

        packed = q_in[source].astype(f32)
        low = lax.broadcasted_iota(jnp.int32, packed.shape, 1) < 64
        top = jnp.where(low, packed, 0.0).astype(bf16)
        bottom = jnp.where(low, pltpu.roll(packed, 64, 1), 0.0).astype(bf16)
        queries = jnp.concatenate((top, bottom), axis=0)
        results = []
        for r in range(sub_rows // BLOCK):
            block = source * (rows // BLOCK) + my_sub * (sub_rows // BLOCK) + r
            picked = [memory[cols_ref[block, j]] for j in range(slots)]
            kv = jnp.concatenate(picked + [global_kv[...]], axis=0)
            scores = lax.dot_general(
                queries[r * BLOCK : (r + 1) * BLOCK],
                kv,
                (((1,), (1,)), ((), ())),
                preferred_element_type=f32,
            )
            weights = jnp.exp(scores + bias[pl.ds(block, 1), :])
            totals = jnp.sum(weights, axis=1, keepdims=True)
            scale = jnp.where(totals > 1.0, 2.0**-10, 1.0)
            probs = (weights * (1.0 / (totals * scale))).astype(bf16)
            results.append(jnp.dot(probs, kv, preferred_element_type=f32) * scale)
        result = jnp.concatenate(results, axis=0)
        top, bottom = result[:half], result[half:]
        o_out[source] = jnp.where(low, pltpu.roll(top, 64, 1), bottom).astype(bf16)

        @pl.when(source != me)
        def _():
            o_copy(source, me).start()

        return carry

    lax.fori_loop(0, n, serve, 0)
    o_in[me] = o_out[me]

    def settle(step, carry):
        peer = (me + step) % n
        o_copy(me, peer).wait_recv()
        kv_copy(peer // repeat, peer, me).wait_send()
        q_copy(peer, me).wait_send()
        o_copy(peer, me).wait_send()
        return carry

    lax.fori_loop(1, n, settle, 0)

    for pair in range(HEADS // 2):
        for sub in range(repeat):
            first = o_in[2 * pair * repeat + sub].astype(f32)
            second = o_in[(2 * pair + 1) * repeat + sub].astype(f32)
            top, bottom = swap_halves(first, second)
            at = slice(pair * 128, pair * 128 + 128)
            out_ref[sub * sub_rows : sub * sub_rows + half, at] = top.astype(bf16)
            out_ref[sub * sub_rows + half : (sub + 1) * sub_rows, at] = bottom.astype(bf16)


def attend(features, gain, weight, used, global_nodes, columns):
    n = lax.axis_size("seq")
    repeat = n // HEADS
    rows, width = features.shape
    half = rows // repeat // 2
    globals_count = global_nodes.shape[0]
    keys = columns.shape[1] * BLOCK + globals_count
    bf16 = jnp.bfloat16
    vmem = pl.BlockSpec(memory_space=pltpu.VMEM)
    flops = 2 * rows * width * 3 * width + 4 * rows * HEADS * 64 * keys
    return pl.pallas_call(
        functools.partial(attention_kernel, n, repeat),
        out_shape=jax.ShapeDtypeStruct((rows, width), bf16),
        in_specs=[vmem] * 6 + [pl.BlockSpec(memory_space=pltpu.SMEM)],
        out_specs=vmem,
        scratch_shapes=[
            pltpu.VMEM((rows, width), bf16),
            pltpu.VMEM((HEADS, rows // BLOCK, BLOCK, 128), bf16),
            pltpu.VMEM((n * rows // BLOCK, BLOCK, 128), bf16),
            pltpu.VMEM((n, half, 128), bf16),
            pltpu.VMEM((n, half, 128), bf16),
            pltpu.VMEM((n, half, 128), bf16),
            pltpu.VMEM((n, half, 128), bf16),
            pltpu.VMEM((globals_count, 128), jnp.float32),
            pltpu.VMEM((globals_count, 128), bf16),
            pltpu.VMEM((columns.shape[0], keys), jnp.float32),
        ]
        + [pltpu.SemaphoreType.DMA((n,))] * 6,
        compiler_params=pltpu.CompilerParams(
            collective_id=0, has_side_effects=True, vmem_limit_bytes=48 * 2**20
        ),
        cost_estimate=pl.CostEstimate(
            flops=flops * 16, bytes_accessed=2**24, transcendentals=rows * HEADS * keys
        ),
        name="attend",
    )(features, gain[None, :], weight, used, global_nodes[None, :], global_nodes[:, None], columns)


def on_device(
    features,
    attention_gain,
    qkv_weight,
    out_weight,
    mlp_gain,
    up_weight,
    down_weight,
    block_columns,
    block_counts,
    global_nodes,
):
    slots = block_columns.shape[1]
    in_list = jnp.arange(slots, dtype=jnp.int32)[None, :] < block_counts[:, None]
    used = jnp.where(in_list, block_columns, -1)
    groups = lax.axis_size("groups")
    part = up_weight.shape[1] // groups
    first = lax.axis_index("groups") * part
    shard = jnp.concatenate(
        (
            lax.dynamic_slice_in_dim(up_weight.T, first, part, 0)[None],
            lax.dynamic_slice_in_dim(down_weight, first, part, 0)[None],
        ),
        axis=0,
    )
    gathered = lax.all_gather(shard, ("seq", "groups"), axis=1, tiled=True)
    up_rows, down_rows = gathered[0], gathered[1]
    attended_rows = attend(
        features, attention_gain, qkv_weight, used, global_nodes, block_columns
    )
    mixed_rows = features.astype(jnp.float32) + jnp.dot(
        attended_rows, out_weight, preferred_element_type=jnp.float32
    )
    normed_mlp = layer_norm(mixed_rows, mlp_gain).astype(jnp.bfloat16)
    hidden = jax.nn.gelu(
        lax.dot_general(
            normed_mlp,
            up_rows,
            (((1,), (1,)), ((), ())),
            preferred_element_type=jnp.float32,
        ),
        approximate=True,
    ).astype(jnp.bfloat16)
    reduced = jnp.dot(
        hidden,
        down_rows,
        preferred_element_type=jnp.float32,
    )
    return (mixed_rows + reduced).astype(jnp.bfloat16)


def solution(mesh):
    in_specs = (
        P(("groups", "seq"), None),
        P(),
        P(),
        P(),
        P(),
        P(None, "seq"),
        P("seq", None),
        P("groups", None),
        P("groups"),
        P("groups"),
    )
    out_specs = P(("groups", "seq"), None)
    return jax.shard_map(
        on_device, mesh=mesh, in_specs=in_specs, out_specs=out_specs, check_vma=False
    )
```

```python
import functools

import jax
import jax.numpy as jnp
from jax import lax
from jax.experimental import pallas as pl
from jax.experimental.pallas import tpu as pltpu
from jax.sharding import PartitionSpec as P

HEADS = 16
BLOCK = 128
EPS = 1e-05
MASKED = -1e30


def layer_norm(values, gain):
    values = values.astype(jnp.float32)
    average = jnp.mean(values, axis=-1, keepdims=True)
    centered = values - average
    variance = jnp.mean(centered * centered, axis=-1, keepdims=True)
    return centered * lax.rsqrt(variance + EPS) * gain


def swap_halves(left, right):
    low = lax.broadcasted_iota(jnp.int32, left.shape, 1) < 64
    return (
        jnp.where(low, left, pltpu.roll(right, 64, 1)),
        jnp.where(low, pltpu.roll(left, 64, 1), right),
    )


def attention_kernel(
    n,
    repeat,
    x_ref,
    gain_ref,
    w_ref,
    used_ref,
    spots_ref,
    gidx_ref,
    cols_ref,
    out_ref,
    normed,
    kv_out,
    memory,
    q_out,
    q_in,
    o_out,
    o_in,
    global_sum,
    global_kv,
    bias,
    kv_send,
    kv_recv,
    q_send,
    q_recv,
    o_send,
    o_recv,
):
    rows, width = x_ref.shape
    sub_rows = rows // repeat
    half = sub_rows // 2
    blocks = rows // BLOCK
    slots = cols_ref.shape[1]
    me = lax.axis_index("seq")
    my_head, my_sub = me // repeat, me % repeat
    f32, bf16 = jnp.float32, jnp.bfloat16

    barrier = pltpu.get_barrier_semaphore()

    def greet(step, carry):
        peer = (me + step) % n
        pl.semaphore_signal(
            barrier, inc=1, device_id={"seq": peer}, device_id_type=pl.DeviceIdType.MESH
        )
        return carry

    lax.fori_loop(1, n, greet, 0)

    def kv_copy(head, owner, source):
        return pltpu.make_async_remote_copy(
            src_ref=kv_out.at[head],
            dst_ref=memory.at[pl.ds(source * blocks, blocks)],
            send_sem=kv_send.at[owner],
            recv_sem=kv_recv.at[source],
            device_id={"seq": owner},
            device_id_type=pl.DeviceIdType.MESH,
        )

    def q_copy(owner, source):
        return pltpu.make_async_remote_copy(
            src_ref=q_out.at[owner],
            dst_ref=q_in.at[source],
            send_sem=q_send.at[owner],
            recv_sem=q_recv.at[source],
            device_id={"seq": owner},
            device_id_type=pl.DeviceIdType.MESH,
        )

    def o_copy(home, worker):
        return pltpu.make_async_remote_copy(
            src_ref=o_out.at[home],
            dst_ref=o_in.at[worker],
            send_sem=o_send.at[home],
            recv_sem=o_recv.at[worker],
            device_id={"seq": home},
            device_id_type=pl.DeviceIdType.MESH,
        )

    def norm_rows(i, carry):
        at = pl.ds(pl.multiple_of(i * BLOCK, BLOCK), BLOCK)
        normed[at, :] = layer_norm(x_ref[at, :], gain_ref[...]).astype(bf16)
        return carry

    lax.fori_loop(0, rows // BLOCK, norm_rows, 0)
    pl.semaphore_wait(barrier, n - 1)

    def quad_of(i):
        return (me // (4 * repeat) + 2 + 3 * i) % (HEADS // 4)

    def project(first, quad):
        columns = pl.ds(pl.multiple_of(first * width + quad * 256, 256), 256)
        return jnp.dot(normed[...], w_ref[:, columns], preferred_element_type=f32)

    def kv_quad(i, carry):
        quad = quad_of(i)
        keys = project(1, quad)
        values = project(2, quad)
        for pair in range(2):
            at = slice(pair * 128, pair * 128 + 128)
            first, second = swap_halves(keys[:, at], values[:, at])
            kv_out[quad * 4 + 2 * pair] = first.astype(bf16).reshape(blocks, BLOCK, 128)
            kv_out[quad * 4 + 2 * pair + 1] = second.astype(bf16).reshape(blocks, BLOCK, 128)
        for inner in range(4):
            head = quad * 4 + inner
            for sub in range(repeat):
                owner = head * repeat + sub

                @pl.when(owner != me)
                def _():
                    kv_copy(head, owner, me).start()

        return carry

    lax.fori_loop(0, HEADS // 4, kv_quad, 0)

    def q_quad(i, carry):
        quad = quad_of(i)
        queries = project(0, quad) * 0.125
        for pair in range(2):
            both = queries[:, pair * 128 : pair * 128 + 128]
            for sub in range(repeat):
                top = both[sub * sub_rows : sub * sub_rows + half]
                bottom = both[sub * sub_rows + half : (sub + 1) * sub_rows]
                first, second = swap_halves(top, bottom)
                head = quad * 4 + 2 * pair
                q_out[head * repeat + sub] = first.astype(bf16)
                q_out[(head + 1) * repeat + sub] = second.astype(bf16)
        for inner in range(4):
            for sub in range(repeat):
                owner = (quad * 4 + inner) * repeat + sub

                @pl.when(owner != me)
                def _():
                    q_copy(owner, me).start()

        return carry

    lax.fori_loop(0, HEADS // 4, q_quad, 0)

    memory[pl.ds(me * blocks, blocks)] = kv_out[my_head]
    q_in[me] = q_out[me]

    used = used_ref[...]
    global_block = lax.shift_right_logical(spots_ref[...], BLOCK.bit_length() - 1)
    excluded = jnp.zeros((used.shape[0], global_block.shape[1]), f32)
    for j in range(slots):
        listed = used[:, j : j + 1]
        excluded = jnp.where(listed == global_block, MASKED, excluded)
        bias[:, j * BLOCK : (j + 1) * BLOCK] = jnp.broadcast_to(
            jnp.where(listed >= 0, 0.0, MASKED), (used.shape[0], BLOCK)
        )
    bias[:, slots * BLOCK :] = excluded

    global_sum[...] = jnp.zeros_like(global_sum)

    def arrive(step, carry):
        source = (me + n // 2 + step) % n

        @pl.when(source != me)
        def _():
            kv_copy(my_head, me, source).wait_recv()

        offset = gidx_ref[...] - source * rows
        spot = lax.broadcasted_iota(jnp.int32, (offset.shape[0], rows), 1)
        chosen = jnp.where(spot == offset, 1.0, 0.0).astype(bf16)
        chunk = memory[pl.ds(source * blocks, blocks)].reshape(rows, 128)
        global_sum[...] += jnp.dot(chosen, chunk, preferred_element_type=f32)
        return carry

    lax.fori_loop(0, n, arrive, 0)
    global_kv[...] = global_sum[...].astype(bf16)

    def serve(step, carry):
        source = (me + n // 2 + step) % n

        @pl.when(source != me)
        def _():
            q_copy(me, source).wait_recv()

        packed = q_in[source].astype(f32)
        low = lax.broadcasted_iota(jnp.int32, packed.shape, 1) < 64
        top = jnp.where(low, packed, 0.0).astype(bf16)
        bottom = jnp.where(low, pltpu.roll(packed, 64, 1), 0.0).astype(bf16)
        queries = jnp.concatenate((top, bottom), axis=0)
        results = []
        for r in range(sub_rows // BLOCK):
            block = source * (rows // BLOCK) + my_sub * (sub_rows // BLOCK) + r
            picked = [memory[cols_ref[block, j]] for j in range(slots)]
            kv = jnp.concatenate(picked + [global_kv[...]], axis=0)
            scores = lax.dot_general(
                queries[r * BLOCK : (r + 1) * BLOCK],
                kv,
                (((1,), (1,)), ((), ())),
                preferred_element_type=f32,
            )
            weights = jnp.exp(scores + bias[pl.ds(block, 1), :])
            totals = jnp.sum(weights, axis=1, keepdims=True)
            scale = jnp.where(totals > 1.0, 2.0**-10, 1.0)
            probs = (weights * (1.0 / (totals * scale))).astype(bf16)
            results.append(jnp.dot(probs, kv, preferred_element_type=f32) * scale)
        result = jnp.concatenate(results, axis=0)
        top, bottom = result[:half], result[half:]
        o_out[source] = jnp.where(low, pltpu.roll(top, 64, 1), bottom).astype(bf16)

        @pl.when(source != me)
        def _():
            o_copy(source, me).start()

        return carry

    lax.fori_loop(0, n, serve, 0)
    o_in[me] = o_out[me]

    def settle(step, carry):
        peer = (me + step) % n
        o_copy(me, peer).wait_recv()
        kv_copy(peer // repeat, peer, me).wait_send()
        q_copy(peer, me).wait_send()
        o_copy(peer, me).wait_send()
        return carry

    lax.fori_loop(1, n, settle, 0)

    for pair in range(HEADS // 2):
        for sub in range(repeat):
            first = o_in[2 * pair * repeat + sub].astype(f32)
            second = o_in[(2 * pair + 1) * repeat + sub].astype(f32)
            top, bottom = swap_halves(first, second)
            at = slice(pair * 128, pair * 128 + 128)
            out_ref[sub * sub_rows : sub * sub_rows + half, at] = top.astype(bf16)
            out_ref[sub * sub_rows + half : (sub + 1) * sub_rows, at] = bottom.astype(bf16)


def attend(features, gain, weight, used, global_nodes, columns):
    n = lax.axis_size("seq")
    repeat = n // HEADS
    rows, width = features.shape
    half = rows // repeat // 2
    globals_count = global_nodes.shape[0]
    keys = columns.shape[1] * BLOCK + globals_count
    bf16 = jnp.bfloat16
    vmem = pl.BlockSpec(memory_space=pltpu.VMEM)
    flops = 2 * rows * width * 3 * width + 4 * rows * HEADS * 64 * keys
    return pl.pallas_call(
        functools.partial(attention_kernel, n, repeat),
        out_shape=jax.ShapeDtypeStruct((rows, width), bf16),
        in_specs=[vmem] * 6 + [pl.BlockSpec(memory_space=pltpu.SMEM)],
        out_specs=vmem,
        scratch_shapes=[
            pltpu.VMEM((rows, width), bf16),
            pltpu.VMEM((HEADS, rows // BLOCK, BLOCK, 128), bf16),
            pltpu.VMEM((n * rows // BLOCK, BLOCK, 128), bf16),
            pltpu.VMEM((n, half, 128), bf16),
            pltpu.VMEM((n, half, 128), bf16),
            pltpu.VMEM((n, half, 128), bf16),
            pltpu.VMEM((n, half, 128), bf16),
            pltpu.VMEM((globals_count, 128), jnp.float32),
            pltpu.VMEM((globals_count, 128), bf16),
            pltpu.VMEM((columns.shape[0], keys), jnp.float32),
        ]
        + [pltpu.SemaphoreType.DMA((n,))] * 6,
        compiler_params=pltpu.CompilerParams(
            collective_id=0, has_side_effects=True, vmem_limit_bytes=48 * 2**20
        ),
        cost_estimate=pl.CostEstimate(
            flops=flops * 16, bytes_accessed=2**24, transcendentals=rows * HEADS * keys
        ),
        name="attend",
    )(features, gain[None, :], weight, used, global_nodes[None, :], global_nodes[:, None], columns)


def on_device(
    features,
    attention_gain,
    qkv_weight,
    out_weight,
    mlp_gain,
    up_weight,
    down_weight,
    block_columns,
    block_counts,
    global_nodes,
):
    slots = block_columns.shape[1]
    in_list = jnp.arange(slots, dtype=jnp.int32)[None, :] < block_counts[:, None]
    used = jnp.where(in_list, block_columns, -1)
    groups = lax.axis_size("groups")
    part = up_weight.shape[1] // groups
    first = lax.axis_index("groups") * part
    shard = jnp.concatenate(
        (
            lax.dynamic_slice_in_dim(up_weight.T, first, part, 0)[None],
            lax.dynamic_slice_in_dim(down_weight, first, part, 0)[None],
        ),
        axis=0,
    )
    gathered = lax.all_gather(shard, ("seq", "groups"), axis=1, tiled=True)
    up_rows, down_rows = gathered[0], gathered[1]
    attended_rows = attend(
        features, attention_gain, qkv_weight, used, global_nodes, block_columns
    )
    mixed_rows = features.astype(jnp.float32) + jnp.dot(
        attended_rows, out_weight, preferred_element_type=jnp.float32
    )
    normed_mlp = layer_norm(mixed_rows, mlp_gain).astype(jnp.bfloat16)
    hidden = jax.nn.gelu(
        lax.dot_general(
            normed_mlp,
            up_rows,
            (((1,), (1,)), ((), ())),
            preferred_element_type=jnp.float32,
        ),
        approximate=True,
    ).astype(jnp.bfloat16)
    reduced = jnp.dot(
        hidden,
        down_rows,
        preferred_element_type=jnp.float32,
    )
    return (mixed_rows + reduced).astype(jnp.bfloat16)


def solution(mesh):
    in_specs = (
        P(("groups", "seq"), None),
        P(),
        P(),
        P(),
        P(),
        P(None, "seq"),
        P("seq", None),
        P("groups", None),
        P("groups"),
        P("groups"),
    )
    out_specs = P(("groups", "seq"), None)
    return jax.shard_map(
        on_device, mesh=mesh, in_specs=in_specs, out_specs=out_specs, check_vma=False
    )
```
